32 devices in a mesh: seq: 8 (over y, x, core), head: 4 (over z).
Axes of the slice: x: 2, y: 2, z: 4, core: 2. Of those that a mesh axis runs over, the one named last changes fastest.
Arguments:
- queries: bfloat16 [1024, 8192], P('seq', 'head'), may hold values from -6 to 6
- keys: bfloat16 [1024, 1024], P('seq'), may hold values from -6 to 6
- values: bfloat16 [1024, 1024], P('seq'), may hold values from -6 to 6
- doc_lengths: int32 [12], replicated, may hold values from 1 to 512, 1024 in all
- fq_weight: bfloat16 [64, 128, 128], P('head'), may hold values from -1 to 1
- fk_weight: bfloat16 [64, 128, 128], P('head'), may hold values from -1 to 1
Outputs:
- residual: float32 [1024, 8192], P('seq', 'head')
- token_loss: float32 [1024], P('seq')
The draws below stay inside these ranges and needn't reach their ends.
Inputs may be any that keep to these rules, and one draw needn't show every extreme that they name: `doc_lengths`: the 12 documents are packed in order and their lengths sum to 1024; the longest has exactly 512 tokens.
All inputs are finite; a program needn't handle non-finite values.
Results may differ from the reference program's by a relative error of at most 0.0035.
Values may be sent and summed in bfloat16 or wider, within the bound.
A program may use at most 64 MiB of HBM per device.

```python
import math
import jax
import jax.numpy as jnp
import numpy as np
from jax import lax

QH = 64
KVH = 8
HD = 128
FH = 128
DOCS = 12
TOKENS = 1024
MAXDOC = 512


def drawn_rows(key, shape):
    return jnp.clip(jax.random.normal(key, shape, jnp.float32), -6.0, 6.0)


def drawn_weight(key, salt):
    bound = min(6.0 * HD ** (-0.5), 1.0)
    drawn = jax.random.normal(jax.random.fold_in(key, salt), (QH, HD, FH), jnp.float32) * HD ** (-0.5)
    return jnp.clip(drawn, -bound, bound)


def draw_queries(key, part):
    result = drawn_rows(key, (TOKENS, QH * HD))
    return result.astype(jnp.bfloat16)


def draw_keys(key, part):
    own_key = jax.random.fold_in(key, 31)
    result = drawn_rows(own_key, (TOKENS, KVH * HD))
    return result.astype(jnp.bfloat16)


def draw_fq_weight(key, part):
    result = drawn_weight(key, 41)
    return result.astype(jnp.bfloat16)


def draw_fk_weight(key, part):
    result = drawn_weight(key, 51)
    return result.astype(jnp.bfloat16)


def steps_of(key, shape, pieces, low, high):
    def one(axis_at, blocks):
        heights = jax.random.uniform(jax.random.fold_in(jax.random.fold_in(key, 6), axis_at), (blocks,), jnp.float32, low / len(pieces), high / len(pieces))
        return jnp.repeat(jnp.exp(heights), shape[axis_at] // blocks).reshape((-1,) + (1,) * (len(shape) - axis_at - 1))

    level = one(*pieces[0])
    for cut in pieces[1:]:
        level = level * one(*cut)
    return level


def profile(amount, total, most, lean):
    loads = [(1 << 20) // math.isqrt(rank ** lean) + 1 for rank in range(2, amount + 1)]
    rest, holding = total - most - (amount - 1), [1] * (amount - 1)
    while rest > 0:
        free = [i for i in range(amount - 1) if holding[i] < most]
        pool, remaining = sum([loads[i] for i in free]), rest
        for i in free:
            more = min(most - holding[i], max(1, remaining * loads[i] // pool), rest)
            holding[i] = holding[i] + more
            rest = rest - more
    return np.array([most] + holding)


def ragged_sizes(stream_key, count, total, most, lean):
    if count == 2:
        one = jax.random.randint(stream_key, (), max(1, total - most), min(most, total - 1) + 1)
        return jnp.stack([one, total - one])
    tallies = jnp.asarray(profile(count, total, most, lean), jnp.int32)
    couples = (count - 1) // 2
    donor, receiver = tallies[1:1 + 2 * couples:2], tallies[2:2 + 2 * couples:2]
    margin = jnp.minimum(donor - 1, most - receiver)
    shifted = jax.random.randint(jax.random.fold_in(stream_key, 1), (couples,), 0, 1 << 20) % (margin + 1)
    tallies = tallies.at[1:1 + 2 * couples:2].set(donor - shifted).at[2:2 + 2 * couples:2].set(receiver + shifted)
    return tallies[jax.random.permutation(jax.random.fold_in(stream_key, 2), count)]


def noise(rng, dims, spread, most, pieces=(), kind=jnp.bfloat16):
    values = spread * jax.random.normal(rng, dims, jnp.float32)
    if pieces:
        values = values * steps_of(rng, dims, pieces, -0.22, 0.18)
    return jnp.clip(values, -most, most).astype(kind)


def setup_inputs(seed: int = 0) -> dict:
    key_list = jax.random.split(jax.random.key(seed), 7)
    return {
        "queries": draw_queries(jax.random.fold_in(key_list[6], 71), 0),
        "keys": draw_keys(jax.random.fold_in(key_list[6], 71), 0),
        "values": noise(key_list[2], (TOKENS, KVH * HD), 1.0, 6.0, ((0, 8),)),
        "doc_lengths": ragged_sizes(key_list[3], DOCS, TOKENS, MAXDOC, 2).astype(jnp.int32),
        "fq_weight": draw_fq_weight(jax.random.fold_in(key_list[6], 71), 0),
        "fk_weight": draw_fk_weight(jax.random.fold_in(key_list[6], 71), 0),
    }


NEG = -1e30


def doc_index(positions, starts):
    return jnp.sum((starts[None, :] <= positions[:, None]).astype(jnp.int32), axis=1) - 1


def feature(inputs, weight):
    proj = jnp.dot(inputs, weight, preferred_element_type=jnp.float32)
    return jnp.concatenate([jax.nn.softmax(proj, axis=-1), jax.nn.softmax(-proj, axis=-1)], axis=-1).astype(jnp.bfloat16)


def head_pass(head, queries, keys, values, starts, fq_weight, fk_weight):
    group = QH // KVH
    q_head = lax.dynamic_slice_in_dim(queries, head * HD, HD, 1)
    k_head = lax.dynamic_slice_in_dim(keys, (head // group) * HD, HD, 1)
    v_head = lax.dynamic_slice_in_dim(values, (head // group) * HD, HD, 1)
    blk = math.gcd(TOKENS, 512)
    span = min(MAXDOC + blk, TOKENS)
    blocks = TOKENS // blk
    scale = HD ** -0.5

    def teacher_block(index):
        q_start = index * blk
        k_start = jnp.clip(q_start + blk - span, 0, TOKENS - span).astype(jnp.int32)
        q_pos = q_start + jnp.arange(blk, dtype=jnp.int32)
        k_pos = k_start + jnp.arange(span, dtype=jnp.int32)
        q_rows = lax.dynamic_slice_in_dim(q_head, q_start, blk, 0)
        k_rows = lax.dynamic_slice_in_dim(k_head, k_start, span, 0)
        v_rows = lax.dynamic_slice_in_dim(v_head, k_start, span, 0)
        mask = (doc_index(q_pos, starts)[:, None] == doc_index(k_pos, starts)[None, :]) & (k_pos[None, :] <= q_pos[:, None])
        scores = jnp.dot(q_rows, k_rows.T, preferred_element_type=jnp.float32) * scale
        scores = jnp.where(mask, scores, NEG)
        peak = jnp.max(scores, axis=1)
        weights = jnp.where(mask, jnp.exp(scores - peak[:, None]), 0.0)
        total = jnp.sum(weights, axis=1)
        return jnp.dot(weights.astype(jnp.bfloat16), v_rows, preferred_element_type=jnp.float32) / total[:, None]

    teacher = lax.map(teacher_block, jnp.arange(blocks, dtype=jnp.int32)).reshape(TOKENS, HD)
    query_feature_map = feature(q_head, fq_weight[head])
    key_feature_map = feature(k_head, fk_weight[head])

    def student_block(carry, index):
        state, norm_state = carry
        q_start = index * blk
        positions = q_start + jnp.arange(blk, dtype=jnp.int32)
        docs = doc_index(positions, starts)
        fq = lax.dynamic_slice_in_dim(query_feature_map, q_start, blk, 0)
        fk = lax.dynamic_slice_in_dim(key_feature_map, q_start, blk, 0)
        v_rows = lax.dynamic_slice_in_dim(v_head, q_start, blk, 0)
        mask = (docs[:, None] == docs[None, :]) & (positions[None, :] <= positions[:, None])
        score_matrix = jnp.where(mask, jnp.dot(fq, fk.T, preferred_element_type=jnp.float32), 0.0)
        numer = jnp.dot(score_matrix, v_rows.astype(jnp.float32), precision=lax.Precision.HIGHEST)
        denom = jnp.sum(score_matrix, axis=1)
        prev_doc = doc_index(jnp.reshape(q_start - 1, (1,)).astype(jnp.int32), starts)[0]
        carried = (docs == prev_doc).astype(jnp.float32)
        fq_wide = fq.astype(jnp.float32)
        numer = numer + carried[:, None] * jnp.dot(fq_wide, state, precision=lax.Precision.HIGHEST)
        denom = denom + carried * jnp.dot(fq_wide, norm_state, precision=lax.Precision.HIGHEST)
        last_mask = (docs == docs[-1]).astype(jnp.bfloat16)
        fk_last = fk * last_mask[:, None]
        inside = jnp.sum(((starts >= q_start) & (starts < q_start + blk)).astype(jnp.int32))
        keep = (inside == 0).astype(jnp.float32)
        state = keep * state + jnp.dot(fk_last.T, v_rows, preferred_element_type=jnp.float32)
        norm_state = keep * norm_state + jnp.sum(fk_last.astype(jnp.float32), axis=0)
        return (state, norm_state), numer / denom[:, None]

    init = (jnp.zeros((2 * FH, HD), jnp.float32), jnp.zeros((2 * FH,), jnp.float32))
    ignored, student = lax.scan(student_block, init, jnp.arange(blocks, dtype=jnp.int32))
    return teacher - student.reshape(TOKENS, HD)


def reference(queries, keys, values, doc_lengths, fq_weight, fk_weight):
    starts = (jnp.cumsum(doc_lengths) - doc_lengths).astype(jnp.int32)
    residuals = lax.map(lambda head: head_pass(head, queries, keys, values, starts, fq_weight, fk_weight), jnp.arange(QH, dtype=jnp.int32))
    residual = jnp.transpose(residuals, (1, 0, 2)).reshape(TOKENS, QH * HD)
    token_loss = jnp.sum(jnp.mean(residuals * residuals, axis=2), axis=0)
    return residual, token_loss
```

```python
import functools

import jax
import jax.numpy as jnp
from jax import lax
from jax.experimental import pallas as pl
from jax.experimental.pallas import tpu as pltpu
from jax.sharding import PartitionSpec as P

QH = 64
KVH = 8
NEG = -1e30
MESH = pl.DeviceIdType.MESH
UNROLL = 2


def kernel(
    n, nh, dl, q_hbm, k_hbm, v_hbm, fq_hbm, fk_hbm, res, loss,
    q, fq, fk, fkt, kv, kt, vx, phiq, acc, peak, qstart, sq, lbuf, lrecv,
    lsem, osem, ssem, rsem, lssem, lrsem,
):
    T = q_hbm.shape[0]
    H, D, F = fq_hbm.shape
    KV = kv.shape[1]
    G = H // KV
    group = QH // KVH
    reach = n // 2
    E = reach // 2
    s = lax.axis_index("seq")
    z = lax.axis_index("head")
    core = lax.rem(s, 2)
    partner = s + 1 - 2 * core
    kv_first = z * H // group
    src = (k_hbm, v_hbm)

    def own(i, g):
        col = pl.multiple_of((kv_first + g) * D, D)
        return src[i].at[:, pl.ds(col, D)]

    load_q = pltpu.make_async_copy(q_hbm, q, lsem.at[0])
    load_fq = pltpu.make_async_copy(fq_hbm, fq, lsem.at[1])
    load_fk = pltpu.make_async_copy(fk_hbm, fk, lsem.at[2])
    own_loads = [
        [pltpu.make_async_copy(own(i, g), kv.at[i, g, 0], osem.at[i, g]) for g in range(KV)]
        for i in range(2)
    ]

    barrier = pltpu.get_barrier_semaphore()
    pl.semaphore_signal(barrier, inc=1, device_id=(partner, z), device_id_type=MESH)
    for e in range(1, E + 1):
        @pl.when(s + 2 * e < n)
        def _():
            pl.semaphore_signal(barrier, inc=1, device_id=(s + 2 * e, z), device_id_type=MESH)

        @pl.when(s - 2 * e >= 0)
        def _():
            pl.semaphore_signal(barrier, inc=1, device_id=(s - 2 * e, z), device_id_type=MESH)
    for e in range(1, nh):
        pl.semaphore_signal(barrier, inc=1, device_id=(s, lax.rem(z + e, nh)), device_id_type=MESH)

    load_q.start()
    load_fq.start()
    load_fk.start()
    for g in range(KV):
        for i in range(2):
            own_loads[i][g].start()

    def direct(i, g, e):
        return pltpu.make_async_remote_copy(
            src_ref=own(i, g), dst_ref=kv.at[i, g, 2 * e],
            send_sem=ssem.at[i, g, 2 * e], recv_sem=rsem.at[i, g, 2 * e],
            device_id=(s + 2 * e, z), device_id_type=MESH)

    def to_partner(i, g):
        return pltpu.make_async_remote_copy(
            src_ref=own(i, g), dst_ref=kv.at[i, g, 1],
            send_sem=ssem.at[i, g, 1], recv_sem=rsem.at[i, g, 1],
            device_id=(partner, z), device_id_type=MESH)

    def relay(i, g, e, k):
        d = 2 * e + 1 - 2 * k
        return pltpu.make_async_remote_copy(
            src_ref=kv.at[i, g, 2 * e], dst_ref=kv.at[i, g, d],
            send_sem=ssem.at[i, g, d], recv_sem=rsem.at[i, g, d],
            device_id=(partner, z), device_id_type=MESH)

    def arrived(i, g, d):
        return pltpu.make_async_remote_copy(
            src_ref=kv.at[i, g, d], dst_ref=kv.at[i, g, d],
            send_sem=ssem.at[i, g, d], recv_sem=rsem.at[i, g, d],
            device_id=(partner, z), device_id_type=MESH)

    anchor = s * T
    qpos = anchor + lax.broadcasted_iota(jnp.int32, (T, 2 * T), 0)
    first = jnp.zeros((T, 2 * T), jnp.int32)
    run = jnp.int32(0)
    for i in range(dl.shape[0]):
        first = jnp.where(qpos >= run, run, first)
        run = run + dl[i]
    qstart[...] = first

    for d in range(1, reach + 1):
        @pl.when(s < d)
        def _():
            kv[:, :, d] = jnp.zeros((2, KV, T, D), kv.dtype)

    pl.semaphore_wait(barrier, 1 + (nh - 1) + jnp.minimum(E, (n - 1 - s) // 2) + jnp.minimum(E, s // 2))

    @pl.when(core == 0)
    def _():
        for g in range(KV):
            for i in range(2):
                to_partner(i, g).start()
    for e in range(1, E + 1):
        @pl.when(s + 2 * e < n)
        def _():
            for g in range(KV):
                for i in range(2):
                    direct(i, g, e).start()

    def qh(h):
        return q[:, pl.ds(pl.multiple_of(h * D, D), D)]

    load_q.wait()
    load_fq.wait()
    load_fk.wait()

    def prepare(h):
        p = jnp.dot(qh(h), fq[h], preferred_element_type=jnp.float32)
        e1 = jnp.exp(p - jnp.max(p, axis=1, keepdims=True))
        e2 = jnp.exp(jnp.min(p, axis=1, keepdims=True) - p)
        e1 = e1 / jnp.sum(e1, axis=1, keepdims=True)
        e2 = e2 / jnp.sum(e2, axis=1, keepdims=True)
        phiq[h] = jnp.concatenate([e1, e2], axis=1).astype(jnp.bfloat16)
        fkt[h] = fk[h].T

    def heads_loop(lo, hi, fn):
        def step(t, c):
            for u in range(UNROLL):
                fn(lo + t * UNROLL + u)
            return c

        lax.fori_loop(0, (hi - lo) // UNROLL, step, 0)

    heads_loop(0, H, prepare)
    sq[...] = jnp.zeros_like(sq)
    c = (D ** -0.5) * 1.4426950408889634

    def chunk(g, ds, last):
        W = T * len(ds)
        initial = ds[0] == 0
        for j, d in enumerate(ds):
            kt[g, :, pl.ds(j * T, T)] = kv[0, g, d].T
            vx[g, pl.ds(j * T, T), pl.ds(0, D)] = kv[1, g, d]
        kpos = lax.broadcasted_iota(jnp.int32, (T, W), 1)
        if initial:
            kpos = kpos + anchor
        else:
            kpos = anchor - ds[0] * T + jnp.where(kpos >= T, kpos - 2 * T, kpos)

        def one(h):
            mask = kpos >= qstart[:, pl.ds(0, W)]
            if initial:
                row = anchor + lax.broadcasted_iota(jnp.int32, (T, W), 0)
                mask = mask & (kpos <= row)
            kth = kt[g, :, pl.ds(0, W)]
            sc = jnp.dot(qh(h), kth, preferred_element_type=jnp.float32)
            sc = jnp.where(mask, sc, NEG)
            top = jnp.max(sc, axis=1, keepdims=True)
            if not initial:
                old = peak[h]
                new = jnp.maximum(old, top)
                factor = jnp.exp2((old - new) * c)
                sub = jnp.concatenate([new, new], axis=1)
            else:
                new = jnp.broadcast_to(top, (T, D))
                sub = new
            w = jnp.exp2((sc - sub) * c).astype(jnp.bfloat16)
            p = jnp.dot(fkt[h], kth, preferred_element_type=jnp.float32)
            e1 = jnp.exp(p - jnp.max(p, axis=0, keepdims=True))
            e2 = jnp.exp(jnp.min(p, axis=0, keepdims=True) - p)
            e1 = e1 * (1.0 / jnp.sum(e1, axis=0, keepdims=True))
            e2 = e2 * (1.0 / jnp.sum(e2, axis=0, keepdims=True))
            phik = jnp.concatenate([e1, e2], axis=0).astype(jnp.bfloat16)
            aff = jnp.dot(phiq[h], phik, preferred_element_type=jnp.float32)
            aff = jnp.where(mask, aff, 0.0).astype(jnp.bfloat16)
            vxg = vx[g, pl.ds(0, W)]
            ot = jnp.dot(w, vxg, preferred_element_type=jnp.float32)
            os = jnp.dot(aff, vxg, preferred_element_type=jnp.float32)
            if not initial:
                ot = ot + acc[h, pl.ds(0, T)] * jnp.concatenate([factor, factor], axis=1)
                os = os + acc[h, pl.ds(T, T)]
            if last:
                r = ot[:, :D] / ot[:, D:] - os[:, :D] / os[:, D:]
                res[:, pl.ds(pl.multiple_of(h * D, D), D)] = r
                sq[...] += r * r
            else:
                peak[h] = new
                acc[h, pl.ds(0, T)] = ot
                acc[h, pl.ds(T, T)] = os

        heads_loop(g * G, (g + 1) * G, one)

    for g in range(KV):
        vx[g, :, pl.ds(D, D)] = jnp.ones((2 * T, D), vx.dtype)
    for g in range(KV):
        for i in range(2):
            own_loads[i][g].wait()
        chunk(g, (0,), False)

    def pass_on(g, e):
        @pl.when(s >= 2 * e)
        def _():
            for i in range(2):
                arrived(i, g, 2 * e).wait_recv()

        for k in range(2):
            if 2 * e + 1 - 2 * k <= reach:
                @pl.when((s >= 2 * e) & (core == k))
                def _():
                    for i in range(2):
                        relay(i, g, e, k).start()

    for e in range(1, E + 1):
        for g in range(KV):
            pass_on(g, e)
        for g in range(KV):
            @pl.when(s >= 2 * e - 1)
            def _():
                for i in range(2):
                    arrived(i, g, 2 * e - 1).wait_recv()
            chunk(g, (2 * e - 1, 2 * e), e == E)

    part = jnp.sum(sq[...].T, axis=0, keepdims=True) * (1.0 / D)
    lbuf[...] = jnp.broadcast_to(part, lbuf.shape)

    def send_loss(e):
        return pltpu.make_async_remote_copy(
            src_ref=lbuf, dst_ref=lrecv.at[e], send_sem=lssem.at[e], recv_sem=lrsem.at[e],
            device_id=(s, lax.rem(z + e, nh)), device_id_type=MESH)

    for e in range(1, nh):
        send_loss(e).start()

    @pl.when(core == 0)
    def _():
        for g in range(KV):
            for i in range(2):
                to_partner(i, g).wait_send()
    for e in range(1, E + 1):
        @pl.when(s + 2 * e < n)
        def _():
            for g in range(KV):
                for i in range(2):
                    direct(i, g, e).wait_send()
        for k in range(2):
            if 2 * e + 1 - 2 * k <= reach:
                @pl.when((s >= 2 * e) & (core == k))
                def _():
                    for g in range(KV):
                        for i in range(2):
                            relay(i, g, e, k).wait_send()
    total = lbuf[0:1]
    for e in range(1, nh):
        send_loss(e).wait_send()
        send_loss(e).wait_recv()
        total = total + lrecv[e, 0:1]
    loss[...] = total


def body(queries, keys, values, doc_lengths, fq_weight, fk_weight):
    n = lax.axis_size("seq")
    nh = lax.axis_size("head")
    T = queries.shape[0]
    H, D, F = fq_weight.shape
    KV = max(1, H // (QH // KVH))
    reach = n // 2
    bf, f32 = jnp.bfloat16, jnp.float32
    hbm = pl.BlockSpec(memory_space=pl.ANY)
    vm = pl.BlockSpec(memory_space=pltpu.VMEM)
    DMA = pltpu.SemaphoreType.DMA
    res, loss = pl.pallas_call(
        functools.partial(kernel, n, nh),
        out_shape=(
            jax.ShapeDtypeStruct((T, H * D), f32),
            jax.ShapeDtypeStruct((1, T), f32),
        ),
        in_specs=[pl.BlockSpec(memory_space=pltpu.SMEM)] + [hbm] * 5,
        out_specs=(vm, vm),
        scratch_shapes=[
            pltpu.VMEM((T, H * D), bf),
            pltpu.VMEM((H, D, F), bf),
            pltpu.VMEM((H, D, F), bf),
            pltpu.VMEM((H, F, D), bf),
            pltpu.VMEM((2, KV, reach + 1, T, D), bf),
            pltpu.VMEM((KV, D, 2 * T), bf),
            pltpu.VMEM((KV, 2 * T, 2 * D), bf),
            pltpu.VMEM((H, T, 2 * F), bf),
            pltpu.VMEM((H, 2 * T, 2 * D), f32),
            pltpu.VMEM((H, T, D), f32),
            pltpu.VMEM((T, 2 * T), jnp.int32),
            pltpu.VMEM((T, D), f32),
            pltpu.VMEM((8, T), f32),
            pltpu.VMEM((nh, 8, T), f32),
            DMA((3,)),
            DMA((2, KV)),
            DMA((2, KV, reach + 1)),
            DMA((2, KV, reach + 1)),
            DMA((nh,)),
            DMA((nh,)),
        ],
        compiler_params=pltpu.CompilerParams(
            collective_id=0, has_side_effects=True, vmem_limit_bytes=40 * 1024 * 1024
        ),
    )(doc_lengths, queries, keys, values, fq_weight, fk_weight)
    return res, loss.reshape(T)


def solution(mesh):
    in_specs = (
        P("seq", "head"),
        P("seq", None),
        P("seq", None),
        P(),
        P("head", None, None),
        P("head", None, None),
    )
    out_specs = (P("seq", "head"), P("seq"))
    return jax.shard_map(body, mesh=mesh, in_specs=in_specs, out_specs=out_specs, check_vma=False)
```

```python
import functools
import math

import jax
import jax.numpy as jnp
from jax import lax
from jax.experimental import pallas as pl
from jax.experimental.pallas import tpu as pltpu
from jax.sharding import PartitionSpec as P

QH = 64
KVH = 8
NEG = -1e30
MESH = pl.DeviceIdType.MESH
UNROLL = 4


def kernel(
    n, nh, dl, q_hbm, k_hbm, v_hbm, fq_hbm, fk_hbm, res, loss,
    q, fq, fk, fkt, kv, kt, vx, phiq, acc, peak, qstart, sq, lbuf, lrecv,
    lsem, osem, ssem, rsem, lssem, lrsem,
):
    T = q_hbm.shape[0]
    H, D, F = fq_hbm.shape
    KV = kv.shape[1]
    G = H // KV
    group = QH // KVH
    reach = n // 2
    E = reach // 2
    s = lax.axis_index("seq")
    z = lax.axis_index("head")
    core = lax.rem(s, 2)
    partner = s + 1 - 2 * core
    kv_first = z * H // group
    src = (k_hbm, v_hbm)

    def own(i, g):
        col = pl.multiple_of((kv_first + g) * D, D)
        return src[i].at[:, pl.ds(col, D)]

    load_q = pltpu.make_async_copy(q_hbm, q, lsem.at[0])
    load_fq = pltpu.make_async_copy(fq_hbm, fq, lsem.at[1])
    load_fk = pltpu.make_async_copy(fk_hbm, fk, lsem.at[2])
    own_loads = [
        [pltpu.make_async_copy(own(i, g), kv.at[i, g, 0], osem.at[i, g]) for g in range(KV)]
        for i in range(2)
    ]

    barrier = pltpu.get_barrier_semaphore()
    pl.semaphore_signal(barrier, inc=1, device_id=(partner, z), device_id_type=MESH)
    for e in range(1, E + 1):
        @pl.when(s + 2 * e < n)
        def _():
            pl.semaphore_signal(barrier, inc=1, device_id=(s + 2 * e, z), device_id_type=MESH)

        @pl.when(s - 2 * e >= 0)
        def _():
            pl.semaphore_signal(barrier, inc=1, device_id=(s - 2 * e, z), device_id_type=MESH)
    for e in range(1, nh):
        pl.semaphore_signal(barrier, inc=1, device_id=(s, lax.rem(z + e, nh)), device_id_type=MESH)

    load_q.start()
    load_fq.start()
    load_fk.start()
    for g in range(KV):
        for i in range(2):
            own_loads[i][g].start()

    def direct(i, g, e):
        return pltpu.make_async_remote_copy(
            src_ref=own(i, g), dst_ref=kv.at[i, g, 2 * e],
            send_sem=ssem.at[i, g, 2 * e], recv_sem=rsem.at[i, g, 2 * e],
            device_id=(s + 2 * e, z), device_id_type=MESH)

    def to_partner(i, g):
        return pltpu.make_async_remote_copy(
            src_ref=own(i, g), dst_ref=kv.at[i, g, 1],
            send_sem=ssem.at[i, g, 1], recv_sem=rsem.at[i, g, 1],
            device_id=(partner, z), device_id_type=MESH)

    def relay(i, g, e, k):
        d = 2 * e + 1 - 2 * k
        return pltpu.make_async_remote_copy(
            src_ref=kv.at[i, g, 2 * e], dst_ref=kv.at[i, g, d],
            send_sem=ssem.at[i, g, d], recv_sem=rsem.at[i, g, d],
            device_id=(partner, z), device_id_type=MESH)

    def arrived(i, g, d):
        return pltpu.make_async_remote_copy(
            src_ref=kv.at[i, g, d], dst_ref=kv.at[i, g, d],
            send_sem=ssem.at[i, g, d], recv_sem=rsem.at[i, g, d],
            device_id=(partner, z), device_id_type=MESH)

    anchor = s * T
    qpos = anchor + lax.broadcasted_iota(jnp.int32, (T, 2 * T), 0)
    first = jnp.zeros((T, 2 * T), jnp.int32)
    run = jnp.int32(0)
    for i in range(dl.shape[0]):
        first = jnp.where(qpos >= run, run, first)
        run = run + dl[i]
    qstart[...] = first

    for d in range(1, reach + 1):
        @pl.when(s < d)
        def _():
            kv[:, :, d] = jnp.zeros((2, KV, T, D), kv.dtype)

    pl.semaphore_wait(barrier, 1 + (nh - 1) + jnp.minimum(E, (n - 1 - s) // 2) + jnp.minimum(E, s // 2))

    @pl.when(core == 0)
    def _():
        for g in range(KV):
            for i in range(2):
                to_partner(i, g).start()
    for e in range(1, E + 1):
        @pl.when(s + 2 * e < n)
        def _():
            for g in range(KV):
                for i in range(2):
                    direct(i, g, e).start()

    def qh(h):
        return q[:, pl.ds(pl.multiple_of(h * D, D), D)]

    load_q.wait()
    load_fq.wait()
    load_fk.wait()

    def prepare(hs):
        ps = [jnp.dot(qh(h), fq[h], preferred_element_type=jnp.float32) for h in hs]
        turned = [fk[h].T for h in hs]
        out = []
        for p in ps:
            e1 = jnp.exp(p - jnp.max(p, axis=1, keepdims=True))
            e2 = jnp.exp(jnp.min(p, axis=1, keepdims=True) - p)
            e1 = e1 * (1.0 / jnp.sum(e1, axis=1, keepdims=True))
            e2 = e2 * (1.0 / jnp.sum(e2, axis=1, keepdims=True))
            out.append(jnp.concatenate([e1, e2], axis=1).astype(jnp.bfloat16))
        for h, t, o in zip(hs, turned, out):
            fkt[h] = t
            phiq[h] = o

    def heads_loop(lo, hi, fn):
        U = math.gcd(UNROLL, hi - lo)

        def step(t, c):
            fn([lo + t * U + u for u in range(U)])
            return c

        lax.fori_loop(0, (hi - lo) // U, step, 0)

    heads_loop(0, H, prepare)
    sq[...] = jnp.zeros_like(sq)
    c = (D ** -0.5) * 1.4426950408889634

    def chunk(g, ds, last):
        W = T * len(ds)
        initial = ds[0] == 0
        for j, d in enumerate(ds):
            kt[g, :, pl.ds(j * T, T)] = kv[0, g, d].T
            vx[g, pl.ds(j * T, T), pl.ds(0, D)] = kv[1, g, d]
        kpos = lax.broadcasted_iota(jnp.int32, (T, W), 1)
        if initial:
            kpos = kpos + anchor
        else:
            kpos = anchor - ds[0] * T + jnp.where(kpos >= T, kpos - 2 * T, kpos)

        def several(hs):
            mask = kpos >= qstart[:, pl.ds(0, W)]
            if initial:
                row = anchor + lax.broadcasted_iota(jnp.int32, (T, W), 0)
                mask = mask & (kpos <= row)
            kth = kt[g, :, pl.ds(0, W)]
            vxg = vx[g, pl.ds(0, W)]
            qs = [qh(h) for h in hs]
            fks = [fkt[h] for h in hs]
            fqs = [phiq[h] for h in hs]
            if not initial:
                olds = [peak[h] for h in hs]
                ats = [acc[h, pl.ds(0, T)] for h in hs]
                ass = [acc[h, pl.ds(T, T)] for h in hs]
            results = []
            for u in range(len(hs)):
                sc = jnp.dot(qs[u], kth, preferred_element_type=jnp.float32)
                p = jnp.dot(fks[u], kth, preferred_element_type=jnp.float32)
                sc = jnp.where(mask, sc, NEG)
                top = jnp.max(sc, axis=1, keepdims=True)
                if not initial:
                    new = jnp.maximum(olds[u], top)
                    factor = jnp.exp2((olds[u] - new) * c)
                    sub = jnp.concatenate([new, new], axis=1)
                else:
                    new = jnp.broadcast_to(top, (T, D))
                    sub = new
                w = jnp.exp2((sc - sub) * c).astype(jnp.bfloat16)
                e1 = jnp.exp(p - jnp.max(p, axis=0, keepdims=True))
                e2 = jnp.exp(jnp.min(p, axis=0, keepdims=True) - p)
                e1 = e1 * (1.0 / jnp.sum(e1, axis=0, keepdims=True))
                e2 = e2 * (1.0 / jnp.sum(e2, axis=0, keepdims=True))
                phik = jnp.concatenate([e1, e2], axis=0).astype(jnp.bfloat16)
                aff = jnp.dot(fqs[u], phik, preferred_element_type=jnp.float32)
                aff = jnp.where(mask, aff, 0.0).astype(jnp.bfloat16)
                ot = jnp.dot(w, vxg, preferred_element_type=jnp.float32)
                os = jnp.dot(aff, vxg, preferred_element_type=jnp.float32)
                if not initial:
                    ot = ot + ats[u] * jnp.concatenate([factor, factor], axis=1)
                    os = os + ass[u]
                if last:
                    results.append(ot[:, :D] / ot[:, D:] - os[:, :D] / os[:, D:])
                else:
                    results.append((new, ot, os))
            if last:
                total = sq[...]
                for h, r in zip(hs, results):
                    res[:, pl.ds(pl.multiple_of(h * D, D), D)] = r
                    total = total + r * r
                sq[...] = total
            else:
                for h, (new, ot, os) in zip(hs, results):
                    peak[h] = new
                    acc[h, pl.ds(0, T)] = ot
                    acc[h, pl.ds(T, T)] = os

        heads_loop(g * G, (g + 1) * G, several)

    for g in range(KV):
        vx[g, :, pl.ds(D, D)] = jnp.ones((2 * T, D), vx.dtype)
    for g in range(KV):
        for i in range(2):
            own_loads[i][g].wait()
        chunk(g, (0,), False)

    def pass_on(g, e):
        @pl.when(s >= 2 * e)
        def _():
            for i in range(2):
                arrived(i, g, 2 * e).wait_recv()

        for k in range(2):
            if 2 * e + 1 - 2 * k <= reach:
                @pl.when((s >= 2 * e) & (core == k))
                def _():
                    for i in range(2):
                        relay(i, g, e, k).start()

    for e in range(1, E + 1):
        for g in range(KV):
            pass_on(g, e)
        for g in range(KV):
            @pl.when(s >= 2 * e - 1)
            def _():
                for i in range(2):
                    arrived(i, g, 2 * e - 1).wait_recv()
            chunk(g, (2 * e - 1, 2 * e), e == E)

    part = jnp.sum(sq[...].T, axis=0, keepdims=True) * (1.0 / D)
    lbuf[...] = jnp.broadcast_to(part, lbuf.shape)

    def send_loss(e):
        return pltpu.make_async_remote_copy(
            src_ref=lbuf, dst_ref=lrecv.at[e], send_sem=lssem.at[e], recv_sem=lrsem.at[e],
            device_id=(s, lax.rem(z + e, nh)), device_id_type=MESH)

    for e in range(1, nh):
        send_loss(e).start()

    @pl.when(core == 0)
    def _():
        for g in range(KV):
            for i in range(2):
                to_partner(i, g).wait_send()
    for e in range(1, E + 1):
        @pl.when(s + 2 * e < n)
        def _():
            for g in range(KV):
                for i in range(2):
                    direct(i, g, e).wait_send()
        for k in range(2):
            if 2 * e + 1 - 2 * k <= reach:
                @pl.when((s >= 2 * e) & (core == k))
                def _():
                    for g in range(KV):
                        for i in range(2):
                            relay(i, g, e, k).wait_send()
    total = lbuf[0:1]
    for e in range(1, nh):
        send_loss(e).wait_send()
        send_loss(e).wait_recv()
        total = total + lrecv[e, 0:1]
    loss[...] = total


def body(queries, keys, values, doc_lengths, fq_weight, fk_weight):
    n = lax.axis_size("seq")
    nh = lax.axis_size("head")
    T = queries.shape[0]
    H, D, F = fq_weight.shape
    KV = max(1, H // (QH // KVH))
    reach = n // 2
    bf, f32 = jnp.bfloat16, jnp.float32
    hbm = pl.BlockSpec(memory_space=pltpu.HBM)
    vm = pl.BlockSpec(memory_space=pltpu.VMEM)
    DMA = pltpu.SemaphoreType.DMA
    res, loss = pl.pallas_call(
        functools.partial(kernel, n, nh),
        out_shape=(
            jax.ShapeDtypeStruct((T, H * D), f32),
            jax.ShapeDtypeStruct((1, T), f32),
        ),
        in_specs=[pl.BlockSpec(memory_space=pltpu.SMEM)] + [hbm] * 5,
        out_specs=(vm, vm),
        scratch_shapes=[
            pltpu.VMEM((T, H * D), bf),
            pltpu.VMEM((H, D, F), bf),
            pltpu.VMEM((H, D, F), bf),
            pltpu.VMEM((H, F, D), bf),
            pltpu.VMEM((2, KV, reach + 1, T, D), bf),
            pltpu.VMEM((KV, D, 2 * T), bf),
            pltpu.VMEM((KV, 2 * T, 2 * D), bf),
            pltpu.VMEM((H, T, 2 * F), bf),
            pltpu.VMEM((H, 2 * T, 2 * D), f32),
            pltpu.VMEM((H, T, D), f32),
            pltpu.VMEM((T, 2 * T), jnp.int32),
            pltpu.VMEM((T, D), f32),
            pltpu.VMEM((8, T), f32),
            pltpu.VMEM((nh, 8, T), f32),
            DMA((3,)),
            DMA((2, KV)),
            DMA((2, KV, reach + 1)),
            DMA((2, KV, reach + 1)),
            DMA((nh,)),
            DMA((nh,)),
        ],
        compiler_params=pltpu.CompilerParams(
            collective_id=0, has_side_effects=True, vmem_limit_bytes=67043328
        ),
    )(doc_lengths, queries, keys, values, fq_weight, fk_weight)
    return res, loss.reshape(T)


def solution(mesh):
    in_specs = (
        P("seq", "head"),
        P("seq", None),
        P("seq", None),
        P(),
        P("head", None, None),
        P("head", None, None),
    )
    out_specs = (P("seq", "head"), P("seq"))
    return jax.shard_map(body, mesh=mesh, in_specs=in_specs, out_specs=out_specs, check_vma=False)
```

```python
import functools
import math

import jax
import jax.numpy as jnp
from jax import lax
from jax.experimental import pallas as pl
from jax.experimental.pallas import tpu as pltpu
from jax.sharding import PartitionSpec as P

QH = 64
KVH = 8
NEG = -1e30
MESH = pl.DeviceIdType.MESH
UNROLL = 4
LOG2E = 1.4426950408889634


def kernel(
    n, nh, dl, q_hbm, k_hbm, v_hbm, fq_hbm, fk_hbm, res, loss,
    q, fq, fk, fkt, kv, kt, vx, phiq, scores, affin, peak, bias, keep, sq, lbuf, lrecv,
    lsem, osem, ssem, rsem, lssem, lrsem,
):
    T = q_hbm.shape[0]
    H, D, F = fq_hbm.shape
    KV = kv.shape[1]
    G = H // KV
    group = QH // KVH
    reach = n // 2
    E = reach // 2
    s = lax.axis_index("seq")
    z = lax.axis_index("head")
    core = lax.rem(s, 2)
    partner = s + 1 - 2 * core
    kv_first = z * H // group
    src = (k_hbm, v_hbm)

    def own(i, g):
        col = pl.multiple_of((kv_first + g) * D, D)
        return src[i].at[:, pl.ds(col, D)]

    load_q = pltpu.make_async_copy(q_hbm, q, lsem.at[0])
    load_fq = pltpu.make_async_copy(fq_hbm, fq, lsem.at[1])
    load_fk = pltpu.make_async_copy(fk_hbm, fk, lsem.at[2])
    own_loads = [
        [pltpu.make_async_copy(own(i, g), kv.at[i, g, 0], osem.at[i, g]) for g in range(KV)]
        for i in range(2)
    ]

    barrier = pltpu.get_barrier_semaphore()
    pl.semaphore_signal(barrier, inc=1, device_id=(partner, z), device_id_type=MESH)
    for e in range(1, E + 1):
        @pl.when(s + 2 * e < n)
        def _():
            pl.semaphore_signal(barrier, inc=1, device_id=(s + 2 * e, z), device_id_type=MESH)

        @pl.when(s - 2 * e >= 0)
        def _():
            pl.semaphore_signal(barrier, inc=1, device_id=(s - 2 * e, z), device_id_type=MESH)
    for e in range(1, nh):
        pl.semaphore_signal(barrier, inc=1, device_id=(s, lax.rem(z + e, nh)), device_id_type=MESH)

    load_q.start()
    load_fq.start()
    load_fk.start()
    for g in range(KV):
        for i in range(2):
            own_loads[i][g].start()

    def direct(i, g, e):
        return pltpu.make_async_remote_copy(
            src_ref=own(i, g), dst_ref=kv.at[i, g, 2 * e],
            send_sem=ssem.at[i, g, 2 * e], recv_sem=rsem.at[i, g, 2 * e],
            device_id=(s + 2 * e, z), device_id_type=MESH)

    def to_partner(i, g):
        return pltpu.make_async_remote_copy(
            src_ref=own(i, g), dst_ref=kv.at[i, g, 1],
            send_sem=ssem.at[i, g, 1], recv_sem=rsem.at[i, g, 1],
            device_id=(partner, z), device_id_type=MESH)

    def relay(i, g, e, k):
        d = 2 * e + 1 - 2 * k
        return pltpu.make_async_remote_copy(
            src_ref=kv.at[i, g, 2 * e], dst_ref=kv.at[i, g, d],
            send_sem=ssem.at[i, g, d], recv_sem=rsem.at[i, g, d],
            device_id=(partner, z), device_id_type=MESH)

    def arrived(i, g, d):
        return pltpu.make_async_remote_copy(
            src_ref=kv.at[i, g, d], dst_ref=kv.at[i, g, d],
            send_sem=ssem.at[i, g, d], recv_sem=rsem.at[i, g, d],
            device_id=(partner, z), device_id_type=MESH)

    anchor = s * T
    row = anchor + lax.broadcasted_iota(jnp.int32, (T, T), 0)
    first = jnp.zeros((T, T), jnp.int32)
    run = jnp.int32(0)
    for i in range(dl.shape[0]):
        first = jnp.where(row >= run, run, first)
        run = run + dl[i]
    for d in range(reach + 1):
        kpos = anchor - d * T + lax.broadcasted_iota(jnp.int32, (T, T), 1)
        mask = kpos >= first
        if d == 0:
            mask = mask & (kpos <= row)
        bias[:, pl.ds(d * T, T)] = jnp.where(mask, 0.0, NEG)
        keep[:, pl.ds(d * T, T)] = jnp.where(mask, 1.0, 0.0).astype(jnp.bfloat16)

    for d in range(1, reach + 1):
        @pl.when(s < d)
        def _():
            kv[:, :, d] = jnp.zeros((2, KV, T, D), kv.dtype)

    pl.semaphore_wait(barrier, 1 + (nh - 1) + jnp.minimum(E, (n - 1 - s) // 2) + jnp.minimum(E, s // 2))

    @pl.when(core == 0)
    def _():
        for g in range(KV):
            for i in range(2):
                to_partner(i, g).start()
    for e in range(1, E + 1):
        @pl.when(s + 2 * e < n)
        def _():
            for g in range(KV):
                for i in range(2):
                    direct(i, g, e).start()

    def qh(h):
        return q[:, pl.ds(pl.multiple_of(h * D, D), D)]

    load_q.wait()
    load_fq.wait()
    load_fk.wait()

    def half(x, axis):
        top = jnp.max(x, axis=axis, keepdims=True)
        low = jnp.min(x, axis=axis, keepdims=True)
        e1 = jnp.exp2(x - top)
        e2 = jnp.exp2(low - x)
        e1 = e1 * (1.0 / jnp.sum(e1, axis=axis, keepdims=True))
        e2 = e2 * (1.0 / jnp.sum(e2, axis=axis, keepdims=True))
        return jnp.concatenate([e1, e2], axis=axis).astype(jnp.bfloat16)

    def heads_loop(lo, hi, fn):
        U = math.gcd(UNROLL, hi - lo)

        def step(t, c):
            fn([lo + t * U + u for u in range(U)])
            return c

        lax.fori_loop(0, (hi - lo) // U, step, 0)

    sq[...] = jnp.zeros_like(sq)
    c = (D ** -0.5) * LOG2E

    def chunk(g, ds):
        W = T * len(ds)
        initial = ds[0] == 0
        at = pl.ds(ds[0] * T, W)
        for j, d in enumerate(ds):
            kt[g, :, pl.ds(j * T, T)] = kv[0, g, d].T
            vx[g, pl.ds(d * T, T), pl.ds(0, D)] = kv[1, g, d]

        def several(hs):
            N = range(len(hs))
            kth = kt[g, :, pl.ds(0, W)]
            qs = [qh(h) for h in hs]
            if initial:
                fks = [fk[h].T for h in hs]
                pq = [jnp.dot(qs[u], fq[hs[u]], preferred_element_type=jnp.float32) for u in N]
            else:
                fks = [fkt[h] for h in hs]
                fqs = [phiq[h] for h in hs]
                tops = [peak[h] for h in hs]
            both = jnp.dot(jnp.concatenate(fks + qs, axis=0), kth, preferred_element_type=jnp.float32)
            if initial:
                fqs = [half(p * LOG2E, 1) for p in pq]
            phiks = [half(both[u * F:(u + 1) * F] * LOG2E, 0) for u in N]
            affs = [jnp.dot(fqs[u], phiks[u], preferred_element_type=jnp.float32) for u in N]
            both = both[len(hs) * F:]
            scs = [both[u * T:(u + 1) * T] + bias[:, at] for u in N]
            news = []
            for u in N:
                new = scs[u][:, :T]
                for j in range(1, len(ds)):
                    new = jnp.maximum(new, scs[u][:, j * T:(j + 1) * T])
                news.append(new if initial else jnp.maximum(new, tops[u]))
            affs = [x.astype(jnp.bfloat16) * keep[:, at] for x in affs]
            for u, h in enumerate(hs):
                if initial:
                    fkt[h] = fks[u]
                    phiq[h] = fqs[u]
                peak[h] = news[u]
                scores[h, :, at] = scs[u]
                affin[h, :, at] = affs[u]

        heads_loop(g * G, (g + 1) * G, several)

    def finish(g):
        def several(hs):
            N = range(len(hs))
            vxg = vx[g]
            tops = [jnp.max(peak[h], axis=1, keepdims=True) for h in hs]
            ws = [jnp.exp2((scores[hs[u]] - tops[u]) * c).astype(jnp.bfloat16) for u in N]
            affs = [affin[h] for h in hs]
            both = jnp.dot(jnp.concatenate(ws + affs, axis=0), vxg, preferred_element_type=jnp.float32)
            ots = [both[u * T:(u + 1) * T] for u in N]
            oss = [both[(len(hs) + u) * T:(len(hs) + u + 1) * T] for u in N]
            results = [ots[u][:, :D] / ots[u][:, D:] - oss[u][:, :D] / oss[u][:, D:] for u in N]
            total = sq[...]
            for h, r in zip(hs, results):
                res[:, pl.ds(pl.multiple_of(h * D, D), D)] = r
                total = total + r * r
            sq[...] = total

        heads_loop(g * G, (g + 1) * G, several)

    for g in range(KV):
        vx[g, :, pl.ds(D, D)] = jnp.ones(((reach + 1) * T, D), vx.dtype)
    for g in range(KV):
        for i in range(2):
            own_loads[i][g].wait()
        chunk(g, (0,))

    def pass_on(g, e):
        @pl.when(s >= 2 * e)
        def _():
            for i in range(2):
                arrived(i, g, 2 * e).wait_recv()

        for k in range(2):
            if 2 * e + 1 - 2 * k <= reach:
                @pl.when((s >= 2 * e) & (core == k))
                def _():
                    for i in range(2):
                        relay(i, g, e, k).start()

    for e in range(1, E + 1):
        for g in range(KV):
            pass_on(g, e)
        for g in range(KV):
            @pl.when(s >= 2 * e - 1)
            def _():
                for i in range(2):
                    arrived(i, g, 2 * e - 1).wait_recv()
            chunk(g, (2 * e - 1, 2 * e))
            if e == E:
                finish(g)

    part = jnp.sum(sq[...].T, axis=0, keepdims=True) * (1.0 / D)
    lbuf[...] = jnp.broadcast_to(part, lbuf.shape)

    def send_loss(e):
        return pltpu.make_async_remote_copy(
            src_ref=lbuf, dst_ref=lrecv.at[e], send_sem=lssem.at[e], recv_sem=lrsem.at[e],
            device_id=(s, lax.rem(z + e, nh)), device_id_type=MESH)

    for e in range(1, nh):
        send_loss(e).start()

    @pl.when(core == 0)
    def _():
        for g in range(KV):
            for i in range(2):
                to_partner(i, g).wait_send()
    for e in range(1, E + 1):
        @pl.when(s + 2 * e < n)
        def _():
            for g in range(KV):
                for i in range(2):
                    direct(i, g, e).wait_send()
        for k in range(2):
            if 2 * e + 1 - 2 * k <= reach:
                @pl.when((s >= 2 * e) & (core == k))
                def _():
                    for g in range(KV):
                        for i in range(2):
                            relay(i, g, e, k).wait_send()
    total = lbuf[0:1]
    for e in range(1, nh):
        send_loss(e).wait_send()
        send_loss(e).wait_recv()
        total = total + lrecv[e, 0:1]
    loss[...] = total


def body(queries, keys, values, doc_lengths, fq_weight, fk_weight):
    n = lax.axis_size("seq")
    nh = lax.axis_size("head")
    T = queries.shape[0]
    H, D, F = fq_weight.shape
    KV = max(1, H // (QH // KVH))
    reach = n // 2
    bf, f32 = jnp.bfloat16, jnp.float32
    hbm = pl.BlockSpec(memory_space=pltpu.HBM)
    vm = pl.BlockSpec(memory_space=pltpu.VMEM)
    DMA = pltpu.SemaphoreType.DMA
    res, loss = pl.pallas_call(
        functools.partial(kernel, n, nh),
        out_shape=(
            jax.ShapeDtypeStruct((T, H * D), f32),
            jax.ShapeDtypeStruct((1, T), f32),
        ),
        in_specs=[pl.BlockSpec(memory_space=pltpu.SMEM)] + [hbm] * 5,
        out_specs=(vm, vm),
        scratch_shapes=[
            pltpu.VMEM((T, H * D), bf),
            pltpu.VMEM((H, D, F), bf),
            pltpu.VMEM((H, D, F), bf),
            pltpu.VMEM((H, F, D), bf),
            pltpu.VMEM((2, KV, reach + 1, T, D), bf),
            pltpu.VMEM((KV, D, 2 * T), bf),
            pltpu.VMEM((KV, (reach + 1) * T, 2 * D), bf),
            pltpu.VMEM((H, T, 2 * F), bf),
            pltpu.VMEM((H, T, (reach + 1) * T), f32),
            pltpu.VMEM((H, T, (reach + 1) * T), bf),
            pltpu.VMEM((H, T, D), f32),
            pltpu.VMEM((T, (reach + 1) * T), f32),
            pltpu.VMEM((T, (reach + 1) * T), bf),
            pltpu.VMEM((T, D), f32),
            pltpu.VMEM((8, T), f32),
            pltpu.VMEM((nh, 8, T), f32),
            DMA((3,)),
            DMA((2, KV)),
            DMA((2, KV, reach + 1)),
            DMA((2, KV, reach + 1)),
            DMA((nh,)),
            DMA((nh,)),
        ],
        compiler_params=pltpu.CompilerParams(
            collective_id=0, has_side_effects=True, vmem_limit_bytes=67043328
        ),
    )(doc_lengths, queries, keys, values, fq_weight, fk_weight)
    return res, loss.reshape(T)


def solution(mesh):
    in_specs = (
        P("seq", "head"),
        P("seq", None),
        P("seq", None),
        P(),
        P("head", None, None),
        P("head", None, None),
    )
    out_specs = (P("seq", "head"), P("seq"))
    return jax.shard_map(body, mesh=mesh, in_specs=in_specs, out_specs=out_specs, check_vma=False)
```

```python
import functools
import math

import jax
import jax.numpy as jnp
from jax import lax
from jax.experimental import pallas as pl
from jax.experimental.pallas import tpu as pltpu
from jax.sharding import PartitionSpec as P

QH = 64
KVH = 8
NEG = -1e30
MESH = pl.DeviceIdType.MESH
UNROLL = 4
LOG2E = 1.4426950408889634


def kernel(
    n, nh, dl, q_hbm, k_hbm, v_hbm, fq_hbm, fk_hbm, res_hbm, loss,
    res, q, fq, fk, fkt, kv, kt, vx, phiq, scores, affin, peak, bias, keep, sq, lbuf, lrecv,
    lsem, osem, ssem, rsem, lssem, lrsem, wsem,
):
    T = q_hbm.shape[0]
    H, D, F = fq_hbm.shape
    KV = kv.shape[1]
    G = H // KV
    group = QH // KVH
    reach = n // 2
    E = reach // 2
    s = lax.axis_index("seq")
    z = lax.axis_index("head")
    core = lax.rem(s, 2)
    partner = s + 1 - 2 * core
    kv_first = z * H // group
    src = (k_hbm, v_hbm)

    def own(i, g):
        col = pl.multiple_of((kv_first + g) * D, D)
        return src[i].at[:, pl.ds(col, D)]

    load_q = pltpu.make_async_copy(q_hbm, q, lsem.at[0])
    load_fq = pltpu.make_async_copy(fq_hbm, fq, lsem.at[1])
    load_fk = pltpu.make_async_copy(fk_hbm, fk, lsem.at[2])
    own_loads = [
        [pltpu.make_async_copy(own(i, g), kv.at[i, g, 0], osem.at[i, g]) for g in range(KV)]
        for i in range(2)
    ]

    barrier = pltpu.get_barrier_semaphore()
    pl.semaphore_signal(barrier, inc=1, device_id=(partner, z), device_id_type=MESH)
    for e in range(1, E + 1):
        @pl.when(s + 2 * e < n)
        def _():
            pl.semaphore_signal(barrier, inc=1, device_id=(s + 2 * e, z), device_id_type=MESH)

        @pl.when(s - 2 * e >= 0)
        def _():
            pl.semaphore_signal(barrier, inc=1, device_id=(s - 2 * e, z), device_id_type=MESH)
    for e in range(1, nh):
        pl.semaphore_signal(barrier, inc=1, device_id=(s, lax.rem(z + e, nh)), device_id_type=MESH)

    load_q.start()
    load_fq.start()
    load_fk.start()
    for g in range(KV):
        for i in range(2):
            own_loads[i][g].start()

    def direct(i, g, e):
        return pltpu.make_async_remote_copy(
            src_ref=own(i, g), dst_ref=kv.at[i, g, 2 * e],
            send_sem=ssem.at[i, g, 2 * e], recv_sem=rsem.at[i, g, 2 * e],
            device_id=(s + 2 * e, z), device_id_type=MESH)

    def to_partner(i, g):
        return pltpu.make_async_remote_copy(
            src_ref=own(i, g), dst_ref=kv.at[i, g, 1],
            send_sem=ssem.at[i, g, 1], recv_sem=rsem.at[i, g, 1],
            device_id=(partner, z), device_id_type=MESH)

    def relay(i, g, e, k):
        d = 2 * e + 1 - 2 * k
        return pltpu.make_async_remote_copy(
            src_ref=kv.at[i, g, 2 * e], dst_ref=kv.at[i, g, d],
            send_sem=ssem.at[i, g, d], recv_sem=rsem.at[i, g, d],
            device_id=(partner, z), device_id_type=MESH)

    def arrived(i, g, d):
        return pltpu.make_async_remote_copy(
            src_ref=kv.at[i, g, d], dst_ref=kv.at[i, g, d],
            send_sem=ssem.at[i, g, d], recv_sem=rsem.at[i, g, d],
            device_id=(partner, z), device_id_type=MESH)

    anchor = s * T
    row = anchor + lax.broadcasted_iota(jnp.int32, (T, T), 0)
    first = jnp.zeros((T, T), jnp.int32)
    run = jnp.int32(0)
    for i in range(dl.shape[0]):
        first = jnp.where(row >= run, run, first)
        run = run + dl[i]
    for d in range(reach + 1):
        kpos = anchor - d * T + lax.broadcasted_iota(jnp.int32, (T, T), 1)
        mask = kpos >= first
        if d == 0:
            mask = mask & (kpos <= row)
        bias[:, pl.ds(d * T, T)] = jnp.where(mask, 0.0, NEG)
        keep[:, pl.ds(d * T, T)] = jnp.where(mask, 1.0, 0.0).astype(jnp.bfloat16)

    for d in range(1, reach + 1):
        @pl.when(s < d)
        def _():
            kv[:, :, d] = jnp.zeros((2, KV, T, D), kv.dtype)

    pl.semaphore_wait(barrier, 1 + (nh - 1) + jnp.minimum(E, (n - 1 - s) // 2) + jnp.minimum(E, s // 2))

    @pl.when(core == 0)
    def _():
        for g in range(KV):
            for i in range(2):
                to_partner(i, g).start()
    for e in range(1, E + 1):
        @pl.when(s + 2 * e < n)
        def _():
            for g in range(KV):
                for i in range(2):
                    direct(i, g, e).start()

    def qh(h):
        return q[:, pl.ds(pl.multiple_of(h * D, D), D)]

    load_q.wait()
    load_fq.wait()
    load_fk.wait()

    def half(x, axis):
        top = jnp.max(x, axis=axis, keepdims=True)
        low = jnp.min(x, axis=axis, keepdims=True)
        e1 = jnp.exp2((x - top) * LOG2E)
        e2 = jnp.exp2((low - x) * LOG2E)
        e1 = e1 * (1.0 / jnp.sum(e1, axis=axis, keepdims=True))
        e2 = e2 * (1.0 / jnp.sum(e2, axis=axis, keepdims=True))
        return jnp.concatenate([e1, e2], axis=axis).astype(jnp.bfloat16)

    def heads_loop(lo, hi, fn):
        U = math.gcd(UNROLL, hi - lo)

        def step(t, c):
            fn([lo + t * U + u for u in range(U)])
            return c

        lax.fori_loop(0, (hi - lo) // U, step, 0)

    sq[...] = jnp.zeros_like(sq)
    c = (D ** -0.5) * LOG2E

    def chunk(g, ds):
        W = T * len(ds)
        initial = ds[0] == 0
        at = pl.ds(ds[0] * T, W)
        for j, d in enumerate(ds):
            kt[g, :, pl.ds(j * T, T)] = kv[0, g, d].T
            vx[g, pl.ds(d * T, T), pl.ds(0, D)] = kv[1, g, d]

        def several(hs):
            N = range(len(hs))
            kth = kt[g, :, pl.ds(0, W)]
            qs = [qh(h) for h in hs]
            if initial:
                fks = [fk[h].T for h in hs]
                pq = [jnp.dot(qs[u], fq[hs[u]], preferred_element_type=jnp.float32) for u in N]
            else:
                fks = [fkt[h] for h in hs]
                fqs = [phiq[h] for h in hs]
                tops = [peak[h] for h in hs]
            both = jnp.dot(jnp.concatenate(fks + qs, axis=0), kth, preferred_element_type=jnp.float32)
            if initial:
                fqs = [half(p, 1) for p in pq]
            phiks = [
                jnp.concatenate([half(both[u * F:(u + 1) * F, j * T:(j + 1) * T], 0) for j in range(len(ds))], axis=1)
                for u in N
            ]
            affs = [jnp.dot(fqs[u], phiks[u], preferred_element_type=jnp.float32) for u in N]
            both = both[len(hs) * F:]
            scs = [both[u * T:(u + 1) * T] + bias[:, at] for u in N]
            news = []
            for u in N:
                new = scs[u][:, :T]
                for j in range(1, len(ds)):
                    new = jnp.maximum(new, scs[u][:, j * T:(j + 1) * T])
                news.append(new if initial else jnp.maximum(new, tops[u]))
            affs = [x.astype(jnp.bfloat16) * keep[:, at] for x in affs]
            for u, h in enumerate(hs):
                if initial:
                    fkt[h] = fks[u]
                    phiq[h] = fqs[u]
                peak[h] = news[u]
                scores[h, :, at] = scs[u]
                affin[h, :, at] = affs[u]

        heads_loop(g * G, (g + 1) * G, several)

    def write_out(g):
        cols = pl.ds(g * G * D, G * D)
        return pltpu.make_async_copy(res.at[:, cols], res_hbm.at[:, cols], wsem.at[g])

    def finish(g):
        def several(hs):
            N = range(len(hs))
            vxg = vx[g]
            tops = [jnp.max(peak[h], axis=1, keepdims=True) for h in hs]
            ws = [jnp.exp2((scores[hs[u]] - tops[u]) * c).astype(jnp.bfloat16) for u in N]
            affs = [affin[h] for h in hs]
            both = jnp.dot(jnp.concatenate(ws + affs, axis=0), vxg, preferred_element_type=jnp.float32)
            ots = [both[u * T:(u + 1) * T] for u in N]
            oss = [both[(len(hs) + u) * T:(len(hs) + u + 1) * T] for u in N]
            results = [ots[u][:, :D] / ots[u][:, D:] - oss[u][:, :D] / oss[u][:, D:] for u in N]
            total = sq[...]
            for h, r in zip(hs, results):
                res[:, pl.ds(pl.multiple_of(h * D, D), D)] = r
                total = total + r * r
            sq[...] = total

        heads_loop(g * G, (g + 1) * G, several)

    for g in range(KV):
        vx[g, :, pl.ds(D, D)] = jnp.ones(((reach + 1) * T, D), vx.dtype)
    for g in range(KV):
        for i in range(2):
            own_loads[i][g].wait()
        chunk(g, (0,))

    def pass_on(g, e):
        @pl.when(s >= 2 * e)
        def _():
            for i in range(2):
                arrived(i, g, 2 * e).wait_recv()

        for k in range(2):
            if 2 * e + 1 - 2 * k <= reach:
                @pl.when((s >= 2 * e) & (core == k))
                def _():
                    for i in range(2):
                        relay(i, g, e, k).start()

    for e in range(1, E + 1):
        for g in range(KV):
            pass_on(g, e)
        for g in range(KV):
            @pl.when(s >= 2 * e - 1)
            def _():
                for i in range(2):
                    arrived(i, g, 2 * e - 1).wait_recv()
            chunk(g, (2 * e - 1, 2 * e))
            if e == E:
                finish(g)
                write_out(g).start()

    part = jnp.sum(sq[...].T, axis=0, keepdims=True) * (1.0 / D)
    lbuf[...] = jnp.broadcast_to(part, lbuf.shape)

    def send_loss(e):
        return pltpu.make_async_remote_copy(
            src_ref=lbuf, dst_ref=lrecv.at[e], send_sem=lssem.at[e], recv_sem=lrsem.at[e],
            device_id=(s, lax.rem(z + e, nh)), device_id_type=MESH)

    for e in range(1, nh):
        send_loss(e).start()

    @pl.when(core == 0)
    def _():
        for g in range(KV):
            for i in range(2):
                to_partner(i, g).wait_send()
    for e in range(1, E + 1):
        @pl.when(s + 2 * e < n)
        def _():
            for g in range(KV):
                for i in range(2):
                    direct(i, g, e).wait_send()
        for k in range(2):
            if 2 * e + 1 - 2 * k <= reach:
                @pl.when((s >= 2 * e) & (core == k))
                def _():
                    for g in range(KV):
                        for i in range(2):
                            relay(i, g, e, k).wait_send()
    total = lbuf[0:1]
    for e in range(1, nh):
        send_loss(e).wait_send()
        send_loss(e).wait_recv()
        total = total + lrecv[e, 0:1]
    loss[...] = total
    for g in range(KV):
        write_out(g).wait()


def body(queries, keys, values, doc_lengths, fq_weight, fk_weight):
    n = lax.axis_size("seq")
    nh = lax.axis_size("head")
    T = queries.shape[0]
    H, D, F = fq_weight.shape
    KV = max(1, H // (QH // KVH))
    reach = n // 2
    bf, f32 = jnp.bfloat16, jnp.float32
    hbm = pl.BlockSpec(memory_space=pltpu.HBM)
    vm = pl.BlockSpec(memory_space=pltpu.VMEM)
    DMA = pltpu.SemaphoreType.DMA
    res, loss = pl.pallas_call(
        functools.partial(kernel, n, nh),
        out_shape=(
            jax.ShapeDtypeStruct((T, H * D), f32),
            jax.ShapeDtypeStruct((1, T), f32),
        ),
        in_specs=[pl.BlockSpec(memory_space=pltpu.SMEM)] + [hbm] * 5,
        out_specs=(hbm, vm),
        scratch_shapes=[
            pltpu.VMEM((T, H * D), f32),
            pltpu.VMEM((T, H * D), bf),
            pltpu.VMEM((H, D, F), bf),
            pltpu.VMEM((H, D, F), bf),
            pltpu.VMEM((H, F, D), bf),
            pltpu.VMEM((2, KV, reach + 1, T, D), bf),
            pltpu.VMEM((KV, D, 2 * T), bf),
            pltpu.VMEM((KV, (reach + 1) * T, 2 * D), bf),
            pltpu.VMEM((H, T, 2 * F), bf),
            pltpu.VMEM((H, T, (reach + 1) * T), f32),
            pltpu.VMEM((H, T, (reach + 1) * T), bf),
            pltpu.VMEM((H, T, D), f32),
            pltpu.VMEM((T, (reach + 1) * T), f32),
            pltpu.VMEM((T, (reach + 1) * T), bf),
            pltpu.VMEM((T, D), f32),
            pltpu.VMEM((8, T), f32),
            pltpu.VMEM((nh, 8, T), f32),
            DMA((3,)),
            DMA((2, KV)),
            DMA((2, KV, reach + 1)),
            DMA((2, KV, reach + 1)),
            DMA((nh,)),
            DMA((nh,)),
            DMA((KV,)),
        ],
        compiler_params=pltpu.CompilerParams(
            collective_id=0, has_side_effects=True, vmem_limit_bytes=67043328
        ),
    )(doc_lengths, queries, keys, values, fq_weight, fk_weight)
    return res, loss.reshape(T)


def solution(mesh):
    in_specs = (
        P("seq", "head"),
        P("seq", None),
        P("seq", None),
        P(),
        P("head", None, None),
        P("head", None, None),
    )
    out_specs = (P("seq", "head"), P("seq"))
    return jax.shard_map(body, mesh=mesh, in_specs=in_specs, out_specs=out_specs, check_vma=False)
```
